32 devices in a mesh: dp: 4 (over y, core), expert: 8 (over z, x).
Axes of the slice: x: 2, y: 2, z: 4, core: 2. Of those that a mesh axis runs over, the one named last changes fastest.
Arguments:
- tokens: bfloat16 [12288, 1024], P(('dp', 'expert')), may hold values from -6 to 6
- cotangent: bfloat16 [12288, 1024], P(('dp', 'expert')), may hold values from -6 to 6
- routes: int32 [12288, 8], P(('dp', 'expert')), may hold values from 0 to 31, all different within a row
- fill_order: int32 [32, 384], P(('dp', 'expert')), may hold values from 0 to 383, each once within a row
- picture_span: int32 [32, 2], P(('dp', 'expert')), may hold values from 0 to 384, as said below
- w_query: bfloat16 [1024, 1024], P('dp'), may hold values from -0.1875 to 0.1875
- w_keyval: bfloat16 [1024, 1024], P('dp'), may hold values from -0.1875 to 0.1875
- w_output: bfloat16 [1024, 1024], P('dp'), may hold values from -1 to 1
- w_router: bfloat16 [1024, 32], P('dp'), may hold values from -0.09375 to 0.09375
- gain_attn: bfloat16 [1024], P('dp'), may hold values from 0.5 to 1.5
- gain_moe: bfloat16 [1024], P('dp'), may hold values from 0.5 to 1.5
- w_gate_up: bfloat16 [32, 1024, 1024], P('expert'), may hold values from -0.1875 to 0.1875
- w_down: bfloat16 [32, 512, 1024], P('expert'), may hold values from -0.75 to 0.75
Outputs:
- output: bfloat16 [12288, 1024], P(('dp', 'expert'))
- grad_tokens: float32 [12288, 1024], P(('dp', 'expert'))
- grad_w_query: float32 [1024, 1024], P('dp')
- grad_w_keyval: float32 [1024, 1024], P('dp')
- grad_w_output: float32 [1024, 1024], P('dp')
- grad_w_router: float32 [1024, 32], P('dp')
- grad_gain_attn: float32 [1024], P('dp')
- grad_gain_moe: float32 [1024], P('dp')
- grad_w_gate_up: float32 [32, 1024, 1024], P('expert')
- grad_w_down: float32 [32, 512, 1024], P('expert')
The draws below stay inside these ranges and needn't reach their ends.
Inputs may be any that keep to these rules, and one draw needn't show every extreme that they name: `routes`: each row names 8 different experts. `fill_order`: each row holds every position of one sequence once. picture_span[s, 1] = picture_span[s, 0] + 256.
All inputs are finite; a program needn't handle non-finite values.
Results may differ from the reference program's by a relative error of at most 0.02.
Values may be sent and summed in bfloat16 or wider, within the bound.
A program may use at most 256 MiB of HBM per device.

```python
import math
import jax
import jax.numpy as jnp
from jax import lax

D = 1024
HEADS = 16
KV_HEADS = 8
HEAD_DIM = 64
EXPERTS = 32
EXP_FF = 512
TOP = 8
PIC = 256
TOK_DEV = 384
SEQS = 32
TOKENS = 12288
QW = 1024
KVW = 1024
CAP = 108


def draw_picture_span(key, part):
    key_start, key_high, key_low = jax.random.split(key, 3)
    starts = jax.random.randint(key_start, (SEQS,), 0, TOK_DEV - PIC + 1, dtype=jnp.int32)
    high_row = jax.random.randint(key_high, (), 0, SEQS, dtype=jnp.int32)
    low_row = (high_row + 1 + jax.random.randint(key_low, (), 0, SEQS - 1, dtype=jnp.int32)) % SEQS
    seq_index = jnp.arange(SEQS, dtype=jnp.int32)
    starts = jnp.where(seq_index == high_row, TOK_DEV - PIC, starts)
    starts = jnp.where(seq_index == low_row, 0, starts)
    return jnp.stack([starts, starts + PIC], axis=1).astype(jnp.int32)


def steps_of(key, extent, pieces, least, top_value):
    factor_of, own = 1.0, jax.random.fold_in(key, 6)
    for dim, blocks in pieces:
        heights = jnp.exp(jax.random.uniform(jax.random.fold_in(own, dim), (blocks,), jnp.float32, least / len(pieces), top_value / len(pieces)))
        factor_of = factor_of * jnp.repeat(heights, extent[dim] // blocks).reshape([-1 if axis == dim else 1 for axis in range(len(extent))])
    return factor_of


def picks_of(own_key, rows, amount, top, lift):
    order = jax.random.permutation(jax.random.fold_in(own_key, 1), amount)
    favour = order
    for power in range(3):
        favour = favour * favour // amount
    favour = favour * lift // amount
    chance = jax.random.randint(jax.random.fold_in(own_key, 2), (rows, amount), 0, 4096) + favour
    sure = jax.random.permutation(jax.random.fold_in(own_key, 3), rows)[jnp.arange(amount) % rows]
    chance = jnp.where(jnp.arange(rows)[:, None] == sure[None, :], 1 << 14, chance)
    score = chance * amount + jnp.arange(amount)
    return lax.top_k(score.astype(jnp.int32), top)[1].astype(jnp.int32)


def scatter_about(key, shape, width, most, cuts=(), kind=jnp.bfloat16):
    gain = steps_of(key, shape, cuts, -0.22, 0.18) if cuts else 1.0
    drawn = jax.random.normal(key, shape, jnp.float32) * width * gain
    return jnp.minimum(jnp.maximum(drawn, -most), most).astype(kind)


def setup_inputs(seed: int = 0) -> dict:
    key_list = jax.random.split(jax.random.key(seed), 14)
    return {
        "tokens": scatter_about(key_list[0], (TOKENS, D), 1.0, 6.0, ((0, 32),)),
        "cotangent": scatter_about(key_list[1], (TOKENS, D), 1.0, 6.0, ((0, 32),)),
        "routes": picks_of(key_list[2], TOKENS, EXPERTS, TOP, 2048),
        "fill_order": jax.vmap(lambda own: jax.random.permutation(own, TOK_DEV))(jax.random.split(key_list[3], SEQS)).reshape((SEQS, TOK_DEV)).astype(jnp.int32),
        "picture_span": draw_picture_span(jax.random.fold_in(key_list[13], 71), 0),
        "w_query": scatter_about(key_list[5], (D, QW), D ** -0.5, 0.1875, ((0, 4),)),
        "w_keyval": scatter_about(key_list[6], (D, KVW), D ** -0.5, 0.1875, ((0, 4),)),
        "w_output": scatter_about(key_list[7], (QW, D), (QW // 32) ** -0.5, 1.0, ((0, 4),)),
        "w_router": scatter_about(key_list[8], (D, EXPERTS), (4 * D) ** -0.5, 0.09375, ((0, 4),)),
        "gain_attn": jnp.clip(1.0 + 0.1 * jax.random.normal(key_list[9], (D,), jnp.float32), 0.5, 1.5).astype(jnp.bfloat16),
        "gain_moe": jnp.clip(1.0 + 0.1 * jax.random.normal(key_list[10], (D,), jnp.float32), 0.5, 1.5).astype(jnp.bfloat16),
        "w_gate_up": scatter_about(key_list[11], (EXPERTS, D, 2 * EXP_FF), D ** -0.5, 0.1875, ((0, 8),)),
        "w_down": scatter_about(key_list[12], (EXPERTS, EXP_FF, D), (EXP_FF // 8) ** -0.5, 0.75, ((0, 8),)),
    }


norm_eps = 1e-05
rope_theta = 10000.0
excluded = -1e+30
highest = lax.Precision.HIGHEST

@jax.custom_vjp
def low(v):
    return lax.optimization_barrier(v.astype(jnp.bfloat16)).astype(jnp.float32)

@jax.custom_vjp
def low_back(v):
    return v

def low_keep(v):
    return (low(v), None)

def low_pass(kept, grad):
    return (grad,)

def back_keep(v):
    return (v, None)

def back_low(kept, grad):
    return (low(grad),)
low.defvjp(low_keep, low_pass)
low_back.defvjp(back_keep, back_low)

def rms_normed(values):
    return values * lax.rsqrt(lax.optimization_barrier(jnp.mean(values * values, axis=-1, keepdims=True)) + norm_eps)

def softmax_rows(values):
    row_max = lax.optimization_barrier(jnp.max(values, axis=-1, keepdims=True))
    powers = jnp.exp(values - row_max)
    return powers / lax.optimization_barrier(jnp.sum(powers, axis=-1, keepdims=True))

def rope_tables(seq_len, head_size):
    half_size = head_size // 2
    exponent = jnp.arange(half_size, dtype=jnp.float32) * (2.0 / head_size)
    frequency = rope_theta ** (-exponent)
    angles = jnp.arange(seq_len, dtype=jnp.float32)[:, None] * frequency[None, :]
    return (jnp.cos(angles), jnp.sin(angles))

def rotate(values, cosine, sine_table):
    half_size = values.shape[-1] // 2
    front_part = values[..., :half_size]
    back_part = values[..., half_size:]
    cos_b = cosine[:, None, :]
    sin_b = sine_table[:, None, :]
    return jnp.concatenate([front_part * cos_b - back_part * sin_b, back_part * cos_b + front_part * sin_b], axis=-1)

def allowed_mask(seq_len, picture):
    position = jnp.arange(seq_len, dtype=jnp.int32)
    causal = position[None, :] <= position[:, None]
    inside = (position >= picture[0]) & (position < picture[1])
    return causal | inside[:, None] & inside[None, :]

def pair_slots(routes_seq, fill_rows):
    ordered = routes_seq[fill_rows].reshape(-1)
    expert_hot = (ordered[:, None] == jnp.arange(EXPERTS, dtype=jnp.int32)[None, :]).astype(jnp.int32)
    running = jnp.cumsum(expert_hot, axis=0, dtype=jnp.int32) - 1
    ordered_slot = lax.optimization_barrier(jnp.sum(running * expert_hot, axis=1, dtype=jnp.int32)).reshape(fill_rows.shape[0], -1)
    return jnp.zeros_like(ordered_slot).at[fill_rows].set(ordered_slot)

def block_forward(inputs, picture, fill_rows, routes_seq, weight_list):
    w_query, w_keyval, w_output, w_router, gain_attn, gain_moe, w_gate_up, w_down = weight_list
    seq_len = inputs.shape[0]
    group_size = HEADS // KV_HEADS
    kv_cols = KV_HEADS * HEAD_DIM
    scale_factor = 1.0 / math.sqrt(HEAD_DIM)
    act_one = low(rms_normed(inputs) * gain_attn)
    query_lin = low_back(jnp.dot(act_one, w_query, precision=highest))
    keyval_lin = low_back(jnp.dot(act_one, w_keyval, precision=highest))
    cosine, sine_table = rope_tables(seq_len, HEAD_DIM)
    queries = low(rotate(query_lin.reshape(seq_len, HEADS, HEAD_DIM), cosine, sine_table))
    queries = queries.reshape(seq_len, KV_HEADS, group_size, HEAD_DIM)
    key_rows = low(rotate(keyval_lin[:, :kv_cols].reshape(seq_len, KV_HEADS, HEAD_DIM), cosine, sine_table))
    values = low(keyval_lin[:, kv_cols:].reshape(seq_len, KV_HEADS, HEAD_DIM))
    raw_scores = low_back(jnp.einsum('qkgd,skd->kgqs', queries, key_rows, precision=highest))
    scores = jnp.where(allowed_mask(seq_len, picture), raw_scores * scale_factor, excluded)
    attention = softmax_rows(scores)
    attended = jnp.einsum('kgqs,skd->qkgd', low(attention), values, precision=highest)
    attended = low(low_back(attended.reshape(seq_len, HEADS * HEAD_DIM)))
    hidden = inputs + low_back(jnp.dot(attended, w_output, precision=highest))
    act_two = low(rms_normed(hidden) * gain_moe)
    logits = low_back(jnp.dot(act_two, w_router, precision=highest))
    chosen = jnp.take_along_axis(logits, routes_seq, axis=1)
    gate_probs = softmax_rows(chosen)
    pair_slot = pair_slots(routes_seq, fill_rows)
    kept_pair = (pair_slot < CAP).astype(gate_probs.dtype)
    flat_expert = routes_seq.reshape(-1)
    flat_slot = pair_slot.reshape(-1)
    dispatch = jnp.zeros((EXPERTS, CAP, inputs.shape[1]), inputs.dtype)
    dispatch = dispatch.at[flat_expert, flat_slot].set(jnp.repeat(act_two, TOP, axis=0), mode='drop')
    dispatch = low_back(dispatch)
    gate_up = low_back(jnp.einsum('ecd,edf->ecf', dispatch, w_gate_up, precision=highest))
    gate_part = gate_up[..., :EXP_FF]
    up_part = gate_up[..., EXP_FF:]
    inner_act = low(gate_part * jax.nn.sigmoid(gate_part) * up_part)
    expert_out = low(low_back(jnp.einsum('ecf,efd->ecd', inner_act, w_down, precision=highest)))
    pair_out = expert_out[flat_expert, jnp.minimum(flat_slot, CAP - 1)].reshape(seq_len, TOP, -1)
    mixture = jnp.einsum('tk,tkd->td', gate_probs * kept_pair, pair_out, precision=highest)
    return hidden + mixture

def reference(tokens, cotangent, routes, fill_order, picture_span, w_query, w_keyval, w_output, w_router, gain_attn, gain_moe, w_gate_up, w_down):
    weights = tuple((matrix.astype(jnp.float32) for matrix in (w_query, w_keyval, w_output, w_router, gain_attn, gain_moe, w_gate_up, w_down)))
    inputs = tokens.astype(jnp.float32).reshape(SEQS, TOK_DEV, D)
    routes_all = routes.reshape(SEQS, TOK_DEV, TOP)

    def forward(inputs_all, weight_list):

        def one_sequence(carried):
            return block_forward(carried[0], carried[1], carried[2], carried[3], weight_list)
        return lax.map(jax.checkpoint(one_sequence), (inputs_all, picture_span, fill_order, routes_all))
    result, pullback = jax.vjp(forward, inputs, weights)
    grad_inputs, grad_weights = pullback(cotangent.astype(jnp.float32).reshape(SEQS, TOK_DEV, D))
    output = result.reshape(TOKENS, D).astype(jnp.bfloat16)
    return (output, grad_inputs.reshape(TOKENS, D), grad_weights[0], grad_weights[1], grad_weights[2], grad_weights[3], grad_weights[4], grad_weights[5], grad_weights[6], grad_weights[7])
```

```python
import functools
import math

import jax
import jax.numpy as jnp
from jax import lax
from jax.experimental import pallas as pl
from jax.experimental.pallas import tpu as pltpu
from jax.sharding import PartitionSpec as P

HEADS = 16
KV_HEADS = 8
HEAD_DIM = 64
EXPERTS = 32
EXP_FF = 512
TOP = 8
CAP = 108
CAP_PAD = 112


norm_eps = 1e-05
rope_theta = 10000.0
excluded = -1e30


def rms_inverse(values):
    return lax.rsqrt(jnp.mean(values * values, axis=-1, keepdims=True) + norm_eps)


def norm_back(grad_act, normed, inverse, gain_vec):
    scaled = grad_act * gain_vec
    gain_grad = jnp.sum(grad_act * normed, axis=0)
    return (
        inverse * (scaled - normed * jnp.mean(scaled * normed, axis=-1, keepdims=True)),
        gain_grad,
    )


def rope_tables(seq_len, head_size):
    half_size = head_size // 2
    exponent = jnp.arange(half_size, dtype=jnp.float32) * (2.0 / head_size)
    frequency = rope_theta ** (-exponent)
    angles = jnp.arange(seq_len, dtype=jnp.float32)[:, None] * frequency[None, :]
    return (jnp.cos(angles), jnp.sin(angles))


def rotate(values, cosine, sine_table):
    half_size = values.shape[-1] // 2
    front_part = values[..., :half_size]
    back_part = values[..., half_size:]
    cos_b = cosine[:, None, :]
    sin_b = sine_table[:, None, :]
    return jnp.concatenate(
        [front_part * cos_b - back_part * sin_b, back_part * cos_b + front_part * sin_b], axis=-1
    )


def allowed_mask(seq_len, picture):
    position = jnp.arange(seq_len, dtype=jnp.int32)
    causal = position[None, :] <= position[:, None]
    inside = (position >= picture[0]) & (position < picture[1])
    return causal | inside[:, None] & inside[None, :]


def slot_table(routes_seq, fill_rows):
    seq_len = fill_rows.shape[0]
    position = jnp.arange(seq_len, dtype=jnp.int32)
    member = jnp.any(
        routes_seq[:, :, None] == jnp.arange(EXPERTS, dtype=jnp.int32)[None, None, :], axis=1
    )
    rank = jnp.sum(
        jnp.where(fill_rows[None, :] == position[:, None], position[None, :], 0), axis=1
    )
    earlier = (rank[None, :] < rank[:, None]).astype(jnp.bfloat16)
    count = jnp.dot(
        earlier, member.astype(jnp.bfloat16), preferred_element_type=jnp.float32
    )
    return jnp.where(member, jnp.minimum(count, float(CAP)), -1.0)


def attention_scores(queries, key_rows, allowed, scale_factor):
    raw_scores = jnp.einsum("qkgd,skd->kgqs", queries, key_rows, preferred_element_type=jnp.float32)
    return jnp.where(allowed, raw_scores * scale_factor, excluded)


def gates_of(acts, router, slots):
    logits = jnp.einsum("...d,de->...e", acts, router, preferred_element_type=jnp.float32)
    member = slots >= 0
    top_value = jnp.max(jnp.where(member, logits, excluded), axis=-1, keepdims=True)
    powers = jnp.where(member, jnp.exp(logits - top_value), 0.0)
    return powers / jnp.sum(powers, axis=-1, keepdims=True)


def fold_order(count):
    return list(range(0, count, 2))[:1] + list(range(1, count, 2)) + list(range(2, count, 2))[::-1]


def pick(table, index):
    value = jnp.int32(table[0])
    for place, entry in enumerate(table[1:], 1):
        value = jnp.where(index == place, jnp.int32(entry), value)
    return value


def ring_of(axis, count):
    me = lax.axis_index(axis)
    half, side = me // 2, me % 2
    order = fold_order(count // 2)
    inverse = [order.index(place) for place in range(count // 2)]
    spot = pick(inverse, half)

    def behind(distance):
        return pick(order, lax.rem(spot - distance + count, count // 2))

    return side, behind


def nt_dot(left, right):
    return lax.dot_general(
        left, right, (((1,), (1,)), ((), ())), preferred_element_type=jnp.float32
    )


def tn_dot(left, right):
    return lax.dot_general(
        left, right, (((0,), (0,)), ((), ())), preferred_element_type=jnp.float32
    )


def plain_dot(left, right):
    return jnp.dot(left, right, preferred_element_type=jnp.float32)


def greet(axis, peers):
    barrier = pltpu.get_barrier_semaphore()
    for peer in peers:
        pl.semaphore_signal(
            barrier, inc=1, device_id={axis: peer}, device_id_type=pl.DeviceIdType.MESH
        )
    pl.semaphore_wait(barrier, len(peers))


def expert_kernel(
    count,
    act_ref,
    dy_ref,
    slot_ref,
    router_ref,
    wgu_ref,
    wdn_ref,
    mix_ref,
    back_ref,
    pair_ref,
    disp_ref,
    inner_ref,
    gug_ref,
    gb_ref,
    xbuf,
    dybuf,
    wgu,
    wdn,
    gates,
    hot_s,
    gate_s,
    disp_s,
    dyr_s,
    inner_s,
    fgate_s,
    fup_s,
    wt_s,
    gb_s,
    gug_s,
    in_s,
    out_s,
    w_sem,
    own_sem,
    dy_sem,
    ring_send,
    ring_recv,
    pair_send,
    pair_recv,
    save_sem,
    out_sem,
):
    local = wgu_ref.shape[0]
    rings = count // 2
    me = lax.axis_index("expert")
    side, behind = ring_of("expert", count)
    nxt = 2 * behind(rings - 1) + side
    prev = 2 * behind(1) + side
    mate = me + 1 - 2 * side
    first = me * local

    load_wgu = pltpu.make_async_copy(wgu_ref, wgu, w_sem.at[0])
    load_wdn = pltpu.make_async_copy(wdn_ref, wdn, w_sem.at[1])
    load_wgu.start()
    pair_ref[...] = jnp.zeros_like(pair_ref)
    load_wdn.start()
    own = pltpu.make_async_copy(act_ref, xbuf.at[0, 0], own_sem)
    own.start()

    def dy_copy(group, lane):
        sequence = 2 * behind(group) + jnp.where(lane == 0, side, 1 - side)
        return pltpu.make_async_copy(
            dy_ref.at[sequence], dybuf.at[lax.rem(group, 2), lane], dy_sem.at[lax.rem(group, 2), lane]
        )

    for lane in range(2):
        dy_copy(0, lane).start()
    own.wait()
    if rings > 2:
        greet("expert", (nxt, prev, mate))
    elif rings == 2:
        greet("expert", (nxt, mate))
    else:
        greet("expert", (mate,))

    def to_next(group):
        return pltpu.make_async_remote_copy(
            src_ref=xbuf.at[group, 0],
            dst_ref=xbuf.at[group + 1, 0],
            send_sem=ring_send.at[group],
            recv_sem=ring_recv.at[group + 1],
            device_id={"expert": nxt},
            device_id_type=pl.DeviceIdType.MESH,
        )

    def to_mate(group):
        return pltpu.make_async_remote_copy(
            src_ref=xbuf.at[group, 0],
            dst_ref=xbuf.at[group, 1],
            send_sem=pair_send.at[group],
            recv_sem=pair_recv.at[group],
            device_id={"expert": mate},
            device_id_type=pl.DeviceIdType.MESH,
        )

    if rings > 1:
        to_next(0).start()
    to_mate(0).start()
    load_wgu.wait()
    load_wdn.wait()

    def saves(group):
        rows = pl.ds(pl.multiple_of(group * 2 * CAP_PAD, 16), 2 * CAP_PAD)
        return [
            pltpu.make_async_copy(disp_s, disp_ref.at[:, rows], save_sem.at[0]),
            pltpu.make_async_copy(inner_s, inner_ref.at[:, rows], save_sem.at[1]),
            pltpu.make_async_copy(gug_s, gug_ref.at[:, rows], save_sem.at[2]),
            pltpu.make_async_copy(gb_s, gb_ref.at[:, rows], save_sem.at[3]),
        ]

    def outs(group, lane):
        sequence = 2 * behind(group) + jnp.where(lane == 0, side, 1 - side)
        return [
            pltpu.make_async_copy(out_s.at[lane, 0], mix_ref.at[sequence], out_sem.at[lane, 0]),
            pltpu.make_async_copy(out_s.at[lane, 1], back_ref.at[sequence], out_sem.at[lane, 1]),
        ]

    slot_iota = lax.broadcasted_iota(jnp.int32, (CAP_PAD, act_ref.shape[0]), 0).astype(jnp.float32)

    def compute(group):
        to_mate(group).wait_recv()
        parity = lax.rem(group, 2)

        @pl.when(group + 1 < rings)
        def _():
            for lane in range(2):
                dy_copy(group + 1, lane).start()

        for lane in range(2):
            dy_copy(group, lane).wait()

        @pl.when(group > 0)
        def _():
            for copy in saves(group - 1):
                copy.wait()

        for lane in range(2):
            sequence = 2 * behind(group) + (side if lane == 0 else 1 - side)
            acts = xbuf[group, lane]
            slots = slot_ref[sequence]
            logits = nt_dot(router_ref[...], acts)
            member = slots >= 0
            top_value = jnp.max(jnp.where(member, logits, excluded), axis=0, keepdims=True)
            powers = jnp.where(member, jnp.exp(logits - top_value), 0.0)
            gates[...] = powers / jnp.sum(powers, axis=0, keepdims=True)
            for e in range(local):
                slot = slot_ref[sequence, pl.ds(first + e, 1), :]
                gate = gates[pl.ds(first + e, 1), :]
                hot = (slot_iota == slot) & (slot < CAP)
                gate_s[e, lane * CAP_PAD : (lane + 1) * CAP_PAD, :] = jnp.sum(
                    jnp.where(hot, gate, 0.0), axis=1, keepdims=True
                )
                hot_s[lane, e * CAP_PAD : (e + 1) * CAP_PAD, :] = jnp.where(hot, 1.0, 0.0).astype(
                    jnp.bfloat16
                )
            rows = plain_dot(hot_s[lane], acts).astype(jnp.bfloat16)
            dy_rows = plain_dot(hot_s[lane], dybuf[parity, lane]).astype(jnp.bfloat16)
            for e in range(local):
                span = slice(lane * CAP_PAD, (lane + 1) * CAP_PAD)
                disp_s[e, span, :] = rows[e * CAP_PAD : (e + 1) * CAP_PAD]
                dyr_s[e, span, :] = dy_rows[e * CAP_PAD : (e + 1) * CAP_PAD]

        def one_expert(e, carry):
            width = act_ref.shape[1]
            ff = wdn.shape[1]
            step = 256
            for n in range(ff // step):
                cols = slice(n * step, (n + 1) * step)
                gate_part = plain_dot(disp_s[e], wgu[e, :, cols])
                up_part = plain_dot(disp_s[e], wgu[e, :, ff + n * step : ff + (n + 1) * step])
                sig = jax.nn.sigmoid(gate_part)
                fup = gate_part * sig
                fup_s[:, cols] = fup
                fgate_s[:, cols] = up_part * sig * (1.0 + gate_part * (1.0 - sig))
                inner_s[e, :, cols] = (fup * up_part).astype(jnp.bfloat16)
            gate_col = gate_s[e]
            pair_col = jnp.zeros_like(gate_col)
            for n in range(width // step):
                cols = slice(n * step, (n + 1) * step)
                made = plain_dot(inner_s[e], wdn[e, :, cols])
                dy_rows = dyr_s[e, :, cols].astype(jnp.float32)
                pair_col = pair_col + jnp.sum(made * dy_rows, axis=1, keepdims=True)
                weighted = (made * gate_col).astype(jnp.bfloat16)
                gb_s[e, :, cols] = (dy_rows * gate_col).astype(jnp.bfloat16)
                for lane in range(2):
                    wt_s[lane, e, :, cols] = weighted[lane * CAP_PAD : (lane + 1) * CAP_PAD]
            for lane in range(2):
                sequence = 2 * behind(group) + (side if lane == 0 else 1 - side)
                hot = hot_s[lane, pl.ds(pl.multiple_of(e * CAP_PAD, 16), CAP_PAD), :]
                pair_ref[sequence, pl.ds(first + e, 1), :] = jnp.sum(
                    hot.astype(jnp.float32) * pair_col[lane * CAP_PAD : (lane + 1) * CAP_PAD],
                    axis=0,
                    keepdims=True,
                )
            for n in range(ff // step):
                cols = slice(n * step, (n + 1) * step)
                grad = nt_dot(gb_s[e], wdn[e, cols, :])
                gug_s[e, :, cols] = (grad * fgate_s[:, cols]).astype(jnp.bfloat16)
                gug_s[e, :, ff + n * step : ff + (n + 1) * step] = (grad * fup_s[:, cols]).astype(
                    jnp.bfloat16
                )
            for n in range(width // step):
                cols = slice(n * step, (n + 1) * step)
                grad = nt_dot(gug_s[e], wgu[e, cols, :]).astype(jnp.bfloat16)
                for lane in range(2):
                    in_s[lane, e, :, cols] = grad[lane * CAP_PAD : (lane + 1) * CAP_PAD]
            return carry

        lax.fori_loop(0, local, one_expert, 0)
        for copy in saves(group):
            copy.start()
        for lane in range(2):

            @pl.when(group > 0)
            def _():
                for copy in outs(group - 1, lane):
                    copy.wait()

            width = act_ref.shape[1]
            flat = (local * CAP_PAD, width)
            out_s[lane, 0] = tn_dot(hot_s[lane], wt_s[lane].reshape(flat)).astype(jnp.bfloat16)
            out_s[lane, 1] = tn_dot(hot_s[lane], in_s[lane].reshape(flat)).astype(jnp.bfloat16)
            for copy in outs(group, lane):
                copy.start()

    def step(group, carry):
        to_next(group - 1).wait_recv()

        @pl.when(group + 1 < rings)
        def _():
            to_next(group).start()

        to_mate(group).start()
        compute(group - 1)
        return carry

    lax.fori_loop(1, rings, step, 0)
    compute(rings - 1)
    for copy in saves(rings - 1) + outs(rings - 1, 0) + outs(rings - 1, 1):
        copy.wait()

    def drain(group, carry):
        to_mate(group).wait_send()

        @pl.when(group + 1 < rings)
        def _():
            to_next(group).wait_send()

        return carry

    lax.fori_loop(0, rings, drain, 0)


def expert_stage(act_two, grads_all, slots_all, router_t, w_gate_up, w_down):
    count, seq_len, width = grads_all.shape
    local, _, wide = w_gate_up.shape
    ff = w_down.shape[1]
    rows = count * CAP_PAD
    group_rows = 2 * CAP_PAD
    bf, f32 = jnp.bfloat16, jnp.float32
    anywhere = pl.BlockSpec(memory_space=pl.ANY)
    vmem = pl.BlockSpec(memory_space=pltpu.VMEM)
    flops = 2 * rows * local * width * ff * 6 + 8 * count * local * CAP_PAD * seq_len * width
    return pl.pallas_call(
        functools.partial(expert_kernel, count),
        out_shape=(
            jax.ShapeDtypeStruct((count, seq_len, width), bf),
            jax.ShapeDtypeStruct((count, seq_len, width), bf),
            jax.ShapeDtypeStruct((count, EXPERTS, seq_len), f32),
            jax.ShapeDtypeStruct((local, rows, width), bf),
            jax.ShapeDtypeStruct((local, rows, ff), bf),
            jax.ShapeDtypeStruct((local, rows, wide), bf),
            jax.ShapeDtypeStruct((local, rows, width), bf),
        ),
        in_specs=[anywhere, anywhere, vmem, vmem, anywhere, anywhere],
        out_specs=(anywhere, anywhere, vmem, anywhere, anywhere, anywhere, anywhere),
        scratch_shapes=[
            pltpu.VMEM((count // 2, 2, seq_len, width), bf),
            pltpu.VMEM((2, 2, seq_len, width), bf),
            pltpu.VMEM((local, width, wide), bf),
            pltpu.VMEM((local, ff, width), bf),
            pltpu.VMEM((EXPERTS, seq_len), f32),
            pltpu.VMEM((2, local * CAP_PAD, seq_len), bf),
            pltpu.VMEM((local, group_rows, 1), f32),
            pltpu.VMEM((local, group_rows, width), bf),
            pltpu.VMEM((local, group_rows, width), bf),
            pltpu.VMEM((local, group_rows, ff), bf),
            pltpu.VMEM((group_rows, ff), f32),
            pltpu.VMEM((group_rows, ff), f32),
            pltpu.VMEM((2, local, CAP_PAD, width), bf),
            pltpu.VMEM((local, group_rows, width), bf),
            pltpu.VMEM((local, group_rows, wide), bf),
            pltpu.VMEM((2, local, CAP_PAD, width), bf),
            pltpu.VMEM((2, 2, seq_len, width), bf),
            pltpu.SemaphoreType.DMA((2,)),
            pltpu.SemaphoreType.DMA,
            pltpu.SemaphoreType.DMA((2, 2)),
            pltpu.SemaphoreType.DMA((count // 2,)),
            pltpu.SemaphoreType.DMA((count // 2,)),
            pltpu.SemaphoreType.DMA((count // 2,)),
            pltpu.SemaphoreType.DMA((count // 2,)),
            pltpu.SemaphoreType.DMA((4,)),
            pltpu.SemaphoreType.DMA((2, 2)),
        ],
        compiler_params=pltpu.CompilerParams(
            collective_id=0, has_side_effects=True, vmem_limit_bytes=60 << 20
        ),
        cost_estimate=pl.CostEstimate(
            flops=flops, bytes_accessed=60 << 20, transcendentals=rows * local * ff
        ),
        name="expert_stage",
    )(act_two, grads_all, slots_all, router_t, w_gate_up, w_down)


def send(src, dst, send_sem, recv_sem, axis, peer):
    return pltpu.make_async_remote_copy(
        src_ref=src,
        dst_ref=dst,
        send_sem=send_sem,
        recv_sem=recv_sem,
        device_id={axis: peer},
        device_id_type=pl.DeviceIdType.MESH,
    )


def neighbours(axis, count):
    rings = count // 2
    side, behind = ring_of(axis, count)
    me = lax.axis_index(axis)
    mate = me + 1 - 2 * side
    nxt = 2 * behind(rings - 1) + side
    prev = 2 * behind(1) + side
    peers = [mate] + ([nxt] if rings > 1 else []) + ([prev] if rings > 2 else [])
    return side, behind, mate, nxt, peers


def greet_all(peers_of):
    barrier = pltpu.get_barrier_semaphore()
    for axis, peers in peers_of:
        for peer in peers:
            pl.semaphore_signal(
                barrier, inc=1, device_id={axis: peer}, device_id_type=pl.DeviceIdType.MESH
            )
    pl.semaphore_wait(barrier, sum(len(peers) for _, peers in peers_of))


class ScatterSum:
    def scratch(count, block, kind):
        rings = count // 2
        deep = min(2, rings)
        return [
            pltpu.VMEM((rings,) + block, kind),
            pltpu.VMEM((rings,) + block, kind),
            pltpu.VMEM((deep,) + block, kind),
            pltpu.VMEM((deep,) + block, kind),
            pltpu.SemaphoreType.DMA((rings,)),
            pltpu.SemaphoreType.DMA((rings,)),
            pltpu.SemaphoreType.DMA((rings,)),
            pltpu.SemaphoreType.DMA((rings,)),
            pltpu.SemaphoreType.DMA((deep,)),
        ]

    def __init__(self, axis, count, part_ref, refs):
        self.axis, self.count, self.part = axis, count, part_ref
        self.rings = count // 2
        self.order = list(range(1, self.rings)) + [0]
        self.side, self.behind, self.mate, self.nxt, _ = neighbours(axis, count)
        (
            self.pair,
            self.ring,
            self.own,
            self.out,
            self.pair_send,
            self.pair_recv,
            self.ring_send,
            self.ring_recv,
            self.own_sem,
        ) = refs

    def to_mate(self, k):
        return send(
            self.part.at[2 * self.behind(k) + 1 - self.side],
            self.pair.at[k],
            self.pair_send.at[k],
            self.pair_recv.at[k],
            self.axis,
            self.mate,
        )

    def to_next(self, k):
        place = (k + 1) % self.rings
        return send(
            self.out.at[k % self.out.shape[0]],
            self.ring.at[place],
            self.ring_send.at[k],
            self.ring_recv.at[place],
            self.axis,
            self.nxt,
        )

    def load(self, at):
        k = self.order[at]
        slot = at % self.own.shape[0]
        return pltpu.make_async_copy(
            self.part.at[2 * self.behind(k) + self.side], self.own.at[slot], self.own_sem.at[slot]
        )

    def begin_load(self):
        for at in range(min(self.own.shape[0], self.rings)):
            self.load(at).start()

    def begin(self):
        for k in self.order:
            self.to_mate(k).start()

    def step(self, at, store=None):
        k = self.order[at]
        slot = at % self.own.shape[0]
        self.load(at).wait()
        self.to_mate(k).wait_recv()
        if at > 0:
            self.to_next((k - 1) % self.rings).wait_recv()
        deep = self.out.shape[0]
        if k >= 1 and k - deep >= 1:
            self.to_next(k - deep).wait_send()
        rows = self.own.shape[1]
        piece = 128 if rows % 128 == 0 and len(self.own.shape) == 3 else rows
        for start in range(0, rows, piece):
            span = slice(start, start + piece)
            value = self.own[slot, span].astype(jnp.float32) + self.pair[k, span].astype(jnp.float32)
            if at > 0:
                value = value + self.ring[k, span].astype(jnp.float32)
            if k == 0:
                store(span, value)
            else:
                self.out[k % deep, span] = value.astype(self.out.dtype)
        if k > 0:
            self.to_next(k).start()
        if at + self.own.shape[0] < self.rings:
            self.load(at + self.own.shape[0]).start()

    def finish(self):
        deep = self.out.shape[0]
        for k in range(max(1, self.rings - deep), self.rings):
            self.to_next(k).wait_send()
        for k in self.order:
            self.to_mate(k).wait_send()


class WholeSum:
    def scratch(count, rows, width):
        rings = count // 2
        steps = max(rings - 1, 1)
        block = (rows, width)
        return [
            pltpu.VMEM((rings,) + block, jnp.bfloat16),
            pltpu.VMEM((steps,) + block, jnp.bfloat16),
            pltpu.VMEM((rings,) + block, jnp.bfloat16),
            pltpu.VMEM((rings,) + block, jnp.bfloat16),
            pltpu.SemaphoreType.DMA((2,)),
            pltpu.SemaphoreType.DMA((steps,)),
            pltpu.SemaphoreType.DMA((steps,)),
            pltpu.SemaphoreType.DMA((steps,)),
            pltpu.SemaphoreType.DMA((rings,)),
            pltpu.SemaphoreType.DMA((rings,)),
            pltpu.SemaphoreType.DMA((rings,)),
        ]

    def __init__(self, axis, count, gw, refs):
        self.axis, self.count, self.gw = axis, count, gw
        self.rings = count // 2
        self.side, self.behind, self.mate, self.nxt, _ = neighbours(axis, count)
        (
            self.got,
            self.ring,
            self.full,
            self.other,
            self.swap_sem,
            self.ring_send,
            self.ring_recv,
            self.back_send,
            self.back_recv,
            self.give_send,
            self.give_recv,
        ) = refs

    def swap(self):
        return send(
            self.gw.at[1 - self.side], self.got, self.swap_sem.at[0], self.swap_sem.at[1], self.axis, self.mate
        )

    def to_next(self, k):
        return send(
            self.got.at[self.behind(k)],
            self.ring.at[k - 1],
            self.ring_send.at[k - 1],
            self.ring_recv.at[k - 1],
            self.axis,
            self.nxt,
        )

    def back(self, g):
        return send(
            self.full.at[g],
            self.full.at[g + 1],
            self.back_send.at[g],
            self.back_recv.at[g + 1],
            self.axis,
            self.nxt,
        )

    def give(self, g):
        return send(
            self.full.at[g], self.other.at[g], self.give_send.at[g], self.give_recv.at[g], self.axis, self.mate
        )

    def begin(self):
        self.swap().start()

    def pair_done(self):
        self.swap().wait_recv()
        for part in range(self.rings):
            total = self.gw[self.side, part].astype(jnp.float32) + self.got[part].astype(jnp.float32)
            self.got[part] = total.astype(jnp.bfloat16)
        if self.rings > 1:
            self.to_next(1).start()

    def ring_done(self):
        for k in range(2, self.rings):
            self.to_next(k - 1).wait_recv()
            part = self.behind(k)
            total = self.got[part].astype(jnp.float32) + self.ring[k - 2].astype(jnp.float32)
            self.got[part] = total.astype(jnp.bfloat16)
            self.to_next(k).start()
        part = self.behind(0)
        total = self.got[part].astype(jnp.float32)
        if self.rings > 1:
            self.to_next(self.rings - 1).wait_recv()
            total = total + self.ring[self.rings - 2].astype(jnp.float32)
        self.full[0] = total.astype(jnp.bfloat16)
        if self.rings > 1:
            self.back(0).start()
        self.give(0).start()

    def back_done(self):
        for g in range(1, self.rings):
            self.back(g - 1).wait_recv()
            if g + 1 < self.rings:
                self.back(g).start()
            self.give(g).start()

    def finish(self):
        self.swap().wait_send()
        for k in range(1, self.rings):
            self.to_next(k).wait_send()
        for g in range(self.rings):
            if g + 1 < self.rings:
                self.back(g).wait_send()
            self.give(g).wait_send()


class Gather:
    def scratch(count):
        rings = count // 2
        return [pltpu.SemaphoreType.DMA((rings,)) for _ in range(4)] + [pltpu.SemaphoreType.DMA]

    def __init__(self, axis, count, own_ref, out_ref, refs):
        self.axis, self.count, self.own, self.out = axis, count, own_ref, out_ref
        self.rings = count // 2
        self.side, self.behind, self.mate, self.nxt, _ = neighbours(axis, count)
        self.ring_send, self.ring_recv, self.pair_send, self.pair_recv, self.own_sem = refs

    def block(self, g):
        return self.own if g == 0 else self.out.at[2 * self.behind(g) + self.side]

    def to_next(self, g):
        return send(
            self.block(g),
            self.out.at[2 * self.behind(g) + self.side],
            self.ring_send.at[g],
            self.ring_recv.at[g + 1],
            self.axis,
            self.nxt,
        )

    def to_mate(self, g):
        return send(
            self.block(g),
            self.out.at[2 * self.behind(g) + self.side],
            self.pair_send.at[g],
            self.pair_recv.at[g],
            self.axis,
            self.mate,
        )

    def keep_own(self):
        return pltpu.make_async_copy(
            self.own, self.out.at[2 * self.behind(0) + self.side], self.own_sem
        )

    def begin(self):
        if self.rings > 1:
            self.to_next(0).start()
        self.to_mate(0).start()
        self.keep_own().start()

    def step(self, g):
        self.to_next(g - 1).wait_recv()
        if g + 1 < self.rings:
            self.to_next(g).start()
        self.to_mate(g).start()

    def finish(self):
        self.keep_own().wait()
        for g in range(self.rings):
            self.to_mate(g).wait_recv()
        for g in range(self.rings):
            self.to_mate(g).wait_send()
            if g + 1 < self.rings:
                self.to_next(g).wait_send()


def weights_kernel(dp_count, count, number, *refs):
    ins, outs, rest = refs[: number + 1], refs[number + 1 : 2 * number + 2], list(refs[2 * number + 2 :])
    gathers = []
    for at in range(number + 1):
        axis, size = ("dp", dp_count) if at < number else ("expert", count)
        gathers.append(Gather(axis, size, ins[at], outs[at], rest[:5]))
        rest = rest[5:]
    greet_all([("dp", neighbours("dp", dp_count)[4]), ("expert", neighbours("expert", count)[4])])
    for gather in gathers:
        gather.begin()
    for g in range(1, max(dp_count, count) // 2):
        for gather in gathers:
            if g < gather.rings:
                gather.step(g)
    for gather in gathers:
        gather.finish()


def weights_stage(blocks, slots, dp_count, count):
    number = len(blocks)
    sizes = [dp_count] * number + [count]
    vmem = pl.BlockSpec(memory_space=pltpu.VMEM)
    anywhere = pl.BlockSpec(memory_space=pl.ANY)
    return pl.pallas_call(
        functools.partial(weights_kernel, dp_count, count, number),
        out_shape=tuple(
            jax.ShapeDtypeStruct((size,) + block.shape, block.dtype)
            for size, block in zip(sizes, list(blocks) + [slots])
        ),
        in_specs=[vmem] * (number + 1),
        out_specs=(anywhere,) * (number + 1),
        scratch_shapes=[ref for size in sizes for ref in Gather.scratch(size)],
        compiler_params=pltpu.CompilerParams(
            collective_id=2, has_side_effects=True, vmem_limit_bytes=16 << 20
        ),
        cost_estimate=pl.CostEstimate(flops=0, bytes_accessed=100 << 20, transcendentals=0),
        name="weights_stage",
    )(*blocks, slots)


def emit_sum(whole, out_ref, sem):
    copies = []
    for g in range(whole.rings):
        part = whole.behind(g)
        copies.append(
            pltpu.make_async_copy(whole.full.at[g], out_ref.at[whole.side, part], sem.at[0, g])
        )
        copies.append(
            pltpu.make_async_copy(whole.other.at[g], out_ref.at[1 - whole.side, part], sem.at[1, g])
        )
    return copies


def scatter_kernel(count, dp_count, sizes, *refs):
    back_ref, pair_ref, disp_ref, inner_ref, gug_ref, gb_ref = refs[:6]
    back_out, pair_out, sum_out, raw_out = refs[6:10]
    rest = list(refs[10:])

    def take(number):
        got, rest[:] = rest[:number], rest[number:]
        return got

    local, early, chunks, chunk, width, ff = sizes
    parts = dp_count // 2
    up_rows, down_rows = width // (2 * parts), ff // (2 * parts)
    back = ScatterSum("expert", count, back_ref, take(9))
    pair = ScatterSum("expert", count, pair_ref, take(9))
    gw_all, load_bufs, load_sem = take(1)[0], take(4), take(1)[0]
    total = take(1)[0] if chunks > 1 else None
    whole = [WholeSum("dp", dp_count, gw_all.at[e], take(11)) for e in range(early)]
    emit_sem, raw_sem = take(2)

    def loads(e, piece, slot):
        rows = pl.ds(pl.multiple_of(piece * chunk, 16), chunk)
        return [
            pltpu.make_async_copy(ref.at[e, rows], buf.at[slot], load_sem.at[slot, i])
            for i, (ref, buf) in enumerate(zip((disp_ref, inner_ref, gug_ref, gb_ref), load_bufs))
        ]

    def weights(e):
        disp, inner, gug, gb = load_bufs

        def products(slot, use):
            for half in range(2):
                for part in range(parts):
                    up_at = (half * parts + part) * up_rows
                    down_at = (half * parts + part) * down_rows
                    use(
                        half,
                        part,
                        tn_dot(disp[slot, :, up_at : up_at + up_rows], gug[slot]),
                        tn_dot(inner[slot, :, down_at : down_at + down_rows], gb[slot]),
                    )

        def keep(half, part, up, down):
            gw_all[e, half, part, :up_rows] = up.astype(jnp.bfloat16)
            gw_all[e, half, part, up_rows:] = down.astype(jnp.bfloat16)

        def gather(half, part, up, down):
            total[half, part, :up_rows] += up
            total[half, part, up_rows:] += down

        if chunks == 1:
            for copy in loads(e, 0, e % 2):
                copy.wait()
            products(e % 2, keep)
            if e + 2 < local:
                for copy in loads(e + 2, 0, e % 2):
                    copy.start()
        else:
            total[...] = jnp.zeros_like(total)

            def one(piece, carry):
                for copy in loads(e, piece, 0):
                    copy.start()
                for copy in loads(e, piece, 0):
                    copy.wait()
                products(0, gather)
                return carry

            lax.fori_loop(0, chunks, one, 0)
            for half in range(2):
                for part in range(parts):
                    gw_all[e, half, part] = total[half, part].astype(jnp.bfloat16)

    def keep_back(span, value):
        back_out[span] = value

    def keep_pair(span, value):
        pair_out[span] = value

    def raw(e):
        return pltpu.make_async_copy(gw_all.at[e], raw_out.at[e - early], raw_sem.at[e - early])

    if chunks == 1:
        for e in range(min(2, local)):
            for copy in loads(e, 0, e):
                copy.start()
    back.begin_load()
    pair.begin_load()
    greet_all([("expert", neighbours("expert", count)[4]), ("dp", neighbours("dp", dp_count)[4])])
    back.begin()
    pair.begin()
    steps = count // 2
    made = 0

    def make(stop):
        nonlocal made
        while made < min(stop, local):
            weights(made)
            if made < early:
                whole[made].begin()
            else:
                raw(made).start()
            made += 1

    make(1)
    make(2)
    whole[0].pair_done()
    for turn in range(steps):
        back.step(turn, keep_back)
        pair.step(turn, keep_pair)
        make(turn + 3)
        if turn + 1 < early:
            whole[turn + 1].pair_done()
        if turn == steps // 2:
            whole[0].ring_done()
    make(local)
    for e in range(steps + 1, early):
        whole[e].pair_done()
    for e in range(1, early):
        whole[e].ring_done()
    for e in range(early):
        whole[e].back_done()
    for e in range(early):
        for g in range(parts):
            whole[e].give(g).wait_recv()
        for copy in emit_sum(whole[e], sum_out.at[e], emit_sem.at[e]):
            copy.start()
    for e in range(early):
        for copy in emit_sum(whole[e], sum_out.at[e], emit_sem.at[e]):
            copy.wait()
    for e in range(early, local):
        raw(e).wait()
    back.finish()
    pair.finish()
    for e in range(early):
        whole[e].finish()


def scatter_stage(back_part, pair_part, disp, inner, gug, gb, dp_count, early):
    count, seq_len, width = back_part.shape
    local, rows, ff = inner.shape
    wide = gug.shape[2]
    bf, f32 = jnp.bfloat16, jnp.float32
    chunk = rows if rows <= 8 * CAP_PAD else 4 * CAP_PAD
    chunks = rows // chunk
    parts = dp_count // 2
    part_rows = (width + ff) // (2 * parts)
    late = max(local - early, 1)
    anywhere = pl.BlockSpec(memory_space=pl.ANY)
    vmem = pl.BlockSpec(memory_space=pltpu.VMEM)
    scratch = (
        ScatterSum.scratch(count, (seq_len, width), bf)
        + ScatterSum.scratch(count, pair_part.shape[1:], f32)
        + [
            pltpu.VMEM((local, 2, parts, part_rows, width), bf),
            pltpu.VMEM((2, chunk, width), bf),
            pltpu.VMEM((2, chunk, ff), bf),
            pltpu.VMEM((2, chunk, wide), bf),
            pltpu.VMEM((2, chunk, width), bf),
            pltpu.SemaphoreType.DMA((2, 4)),
        ]
        + ([pltpu.VMEM((2, parts, part_rows, width), f32)] if chunks > 1 else [])
        + [ref for _ in range(early) for ref in WholeSum.scratch(dp_count, part_rows, width)]
        + [pltpu.SemaphoreType.DMA((early, 2, parts)), pltpu.SemaphoreType.DMA((late,))]
    )
    return pl.pallas_call(
        functools.partial(
            scatter_kernel, count, dp_count, (local, early, chunks, chunk, width, ff)
        ),
        out_shape=(
            jax.ShapeDtypeStruct((seq_len, width), f32),
            jax.ShapeDtypeStruct(pair_part.shape[1:], f32),
            jax.ShapeDtypeStruct((early, 2, parts, part_rows, width), bf),
            jax.ShapeDtypeStruct((late, 2, parts, part_rows, width), bf),
        ),
        in_specs=[anywhere] * 6,
        out_specs=(vmem, vmem, anywhere, anywhere),
        scratch_shapes=scratch,
        compiler_params=pltpu.CompilerParams(
            collective_id=1, has_side_effects=True, vmem_limit_bytes=63 << 20
        ),
        cost_estimate=pl.CostEstimate(
            flops=6 * local * rows * width * ff, bytes_accessed=200 << 20, transcendentals=0
        ),
        name="scatter_stage",
    )(back_part, pair_part, disp, inner, gug, gb)


def shared_kernel(count, dp_count, late, number, *refs):
    grads, raw_ref = refs[:number], refs[number]
    outs, sum_out = refs[number + 1 : 2 * number + 1], refs[2 * number + 1]
    rest = list(refs[2 * number + 2 :])

    def take(amount):
        got, rest[:] = rest[:amount], rest[amount:]
        return got

    firsts, seconds, thirds, mids, fulls = [], [], [], [], []
    for grad in grads:
        mid, own, full = take(3)
        mids.append(mid)
        firsts.append(ScatterSum("dp", dp_count, grad, take(9)))
        seconds.append(ScatterSum("expert", count, mid, take(9)))
        thirds.append((own, Gather("expert", count, own, full, take(5))))
        fulls.append(full)
    whole = []
    if late:
        gw, gw_sem, emit_sem = take(3)
        load = pltpu.make_async_copy(raw_ref, gw, gw_sem)
        load.start()
        whole = [WholeSum("dp", dp_count, gw.at[e], take(11)) for e in range(late)]
    for first in firsts:
        first.begin_load()
    greet_all([("expert", neighbours("expert", count)[4]), ("dp", neighbours("dp", dp_count)[4])])
    for first in firsts:
        first.begin()
    if late:
        load.wait()
    for each in whole:
        each.begin()

    def keep(ref):
        def store(span, value):
            ref[span] = value.astype(ref.dtype)

        return store

    steps, dp_steps = count // 2, dp_count // 2
    for turn in range(dp_steps):
        for first, mid in zip(firsts, mids):
            first.step(turn, keep(mid))
        if turn == 0:
            for each in whole:
                each.pair_done()
    for second in seconds:
        second.begin_load()
        second.begin()
    for turn in range(steps):
        for second, (own, third) in zip(seconds, thirds):
            second.step(turn, keep(own))
        if turn < len(whole):
            whole[turn].ring_done()
    for own, third in thirds:
        third.begin()
    for each in whole[steps:]:
        each.ring_done()
    for g in range(1, steps):
        for own, third in thirds:
            third.step(g)
    for (own, third), full, out in zip(thirds, fulls, outs):
        third.finish()
        out[...] = full[...].astype(jnp.float32)
    for each in whole:
        each.back_done()
    for e, each in enumerate(whole):
        for g in range(each.rings):
            each.give(g).wait_recv()
        for copy in emit_sum(each, sum_out.at[e], emit_sem.at[e]):
            copy.start()
    for e, each in enumerate(whole):
        for copy in emit_sum(each, sum_out.at[e], emit_sem.at[e]):
            copy.wait()
    for each in firsts + seconds + whole:
        each.finish()


def shared_stage(grads, raw, late, count, dp_count):
    bf, f32 = jnp.bfloat16, jnp.float32
    anywhere = pl.BlockSpec(memory_space=pl.ANY)
    vmem = pl.BlockSpec(memory_space=pltpu.VMEM)
    scratch = []
    for grad in grads:
        block = grad.shape[1:]
        scratch += [pltpu.VMEM(block, bf), pltpu.VMEM(block[1:], bf), pltpu.VMEM(block, bf)]
        scratch += ScatterSum.scratch(dp_count, block, bf)
        scratch += ScatterSum.scratch(count, block[1:], bf)
        scratch += Gather.scratch(count)
    if late:
        parts, part_rows, width = raw.shape[2:]
        scratch += [
            pltpu.VMEM(raw.shape, bf),
            pltpu.SemaphoreType.DMA,
            pltpu.SemaphoreType.DMA((late, 2, parts)),
        ]
        scratch += [ref for _ in range(late) for ref in WholeSum.scratch(dp_count, part_rows, width)]
    return pl.pallas_call(
        functools.partial(shared_kernel, count, dp_count, late, len(grads)),
        out_shape=tuple(jax.ShapeDtypeStruct(grad.shape[1:], f32) for grad in grads)
        + (jax.ShapeDtypeStruct(raw.shape, bf),),
        in_specs=[anywhere] * (len(grads) + 1),
        out_specs=(vmem,) * len(grads) + (anywhere,),
        scratch_shapes=scratch,
        compiler_params=pltpu.CompilerParams(
            collective_id=3, has_side_effects=True, vmem_limit_bytes=60 << 20
        ),
        cost_estimate=pl.CostEstimate(flops=0, bytes_accessed=200 << 20, transcendentals=0),
        name="shared_stage",
    )(*grads, raw)


def shards(
    tokens,
    cotangent,
    routes,
    fill_order,
    picture_span,
    w_query,
    w_keyval,
    w_output,
    w_router,
    gain_attn,
    gain_moe,
    w_gate_up,
    w_down,
):
    seq_len, width_model = tokens.shape
    dp_count, count = lax.axis_size("dp"), lax.axis_size("expert")
    small = jnp.concatenate(
        [
            w_router,
            gain_attn[:, None],
            gain_moe[:, None],
            jnp.zeros((w_router.shape[0], 128 - EXPERTS - 2), w_router.dtype),
        ],
        axis=1,
    )
    slots_own = slot_table(routes, fill_order[0])
    small_all, keyval_all, query_all, output_all, slots_all = weights_stage(
        (small, w_keyval, w_query, w_output), slots_own.T, dp_count, count
    )
    small_all, keyval_all, query_all, output_all = (
        each.reshape(-1, each.shape[-1]) for each in (small_all, keyval_all, query_all, output_all)
    )
    router_all = small_all[:, :EXPERTS]
    gain_one = small_all[:, EXPERTS]
    gain_two = small_all[:, EXPERTS + 1]
    grads_all = lax.all_gather(cotangent, "expert", axis=0)
    group_size = HEADS // KV_HEADS
    kv_cols = KV_HEADS * HEAD_DIM
    scale_factor = 1.0 / math.sqrt(HEAD_DIM)
    inputs = tokens.astype(jnp.float32)
    inverse_one = rms_inverse(inputs)
    normed_one = inputs * inverse_one
    gain_one_f = gain_one.astype(jnp.float32)
    act_one = (normed_one * gain_one_f).astype(jnp.bfloat16)
    query_lin = jnp.dot(act_one, query_all, preferred_element_type=jnp.float32)
    keyval_lin = jnp.dot(act_one, keyval_all, preferred_element_type=jnp.float32)
    cosine, sine_table = rope_tables(seq_len, HEAD_DIM)
    queries = rotate(query_lin.reshape(seq_len, HEADS, HEAD_DIM), cosine, sine_table).astype(
        jnp.bfloat16
    )
    queries = queries.reshape(seq_len, KV_HEADS, group_size, HEAD_DIM)
    key_rows = rotate(
        keyval_lin[:, :kv_cols].reshape(seq_len, KV_HEADS, HEAD_DIM), cosine, sine_table
    ).astype(jnp.bfloat16)
    values = keyval_lin[:, kv_cols:].reshape(seq_len, KV_HEADS, HEAD_DIM).astype(jnp.bfloat16)
    allowed = allowed_mask(seq_len, picture_span[0])
    scores = attention_scores(queries, key_rows, allowed, scale_factor)
    row_max = jnp.max(scores, axis=-1, keepdims=True)
    powers = jnp.exp(scores - row_max)
    row_total = jnp.sum(powers, axis=-1, keepdims=True)
    attention = powers / row_total
    log_total = row_max + jnp.log(row_total)
    attended = jnp.einsum(
        "kgqs,skd->qkgd", attention.astype(jnp.bfloat16), values, preferred_element_type=jnp.float32
    )
    attended = attended.reshape(seq_len, HEADS * HEAD_DIM).astype(jnp.bfloat16)
    hidden = inputs + jnp.dot(attended, output_all, preferred_element_type=jnp.float32)
    inverse_two = rms_inverse(hidden)
    normed_two = hidden * inverse_two
    gain_two_f = gain_two.astype(jnp.float32)
    act_two = (normed_two * gain_two_f).astype(jnp.bfloat16)
    mixture_part, back_part, pair_part, disp, inner, gug, gb = expert_stage(
        act_two, grads_all, slots_all, router_all.T, w_gate_up, w_down
    )
    local = w_gate_up.shape[0]
    early = max(local // 2, 1)
    late = local - early
    back, pair_grad, early_sum, raw = scatter_stage(
        back_part, pair_part, disp, inner, gug, gb, dp_count, early
    )
    pair_grad = pair_grad.T
    mixture_part, back = lax.optimization_barrier((mixture_part, back))
    mixture = lax.psum_scatter(
        mixture_part, "expert", scatter_dimension=0, tiled=False
    ).astype(jnp.float32)
    output = (hidden + mixture).astype(jnp.bfloat16)
    gate_own = gates_of(act_two, router_all, slots_own)
    grad_out = cotangent.astype(jnp.float32)
    logit_grad = (
        gate_own * (pair_grad - jnp.sum(gate_own * pair_grad, axis=1, keepdims=True))
    ).astype(jnp.bfloat16)
    act_two_grad = back + jnp.dot(logit_grad, router_all.T, preferred_element_type=jnp.float32)
    grad_router = jnp.dot(act_two.T, logit_grad, preferred_element_type=jnp.float32)
    norm_grad_two, grad_gain_two = norm_back(act_two_grad, normed_two, inverse_two, gain_two_f)
    hidden_grad = grad_out + norm_grad_two
    attn_grad = hidden_grad.astype(jnp.bfloat16)
    grad_output_w = jnp.dot(attended.T, attn_grad, preferred_element_type=jnp.float32)
    attended_grad = jnp.dot(attn_grad, output_all.T, preferred_element_type=jnp.float32).astype(
        jnp.bfloat16
    )
    attended_grad = attended_grad.reshape(seq_len, KV_HEADS, group_size, HEAD_DIM)
    scores_again = attention_scores(queries, key_rows, allowed, scale_factor)
    attention_again = jnp.exp(scores_again - log_total)
    prob_grad = jnp.einsum(
        "qkgd,skd->kgqs", attended_grad, values, preferred_element_type=jnp.float32
    )
    row_dot = jnp.sum(attention_again * prob_grad, axis=-1, keepdims=True)
    score_grad = (attention_again * (prob_grad - row_dot) * scale_factor).astype(jnp.bfloat16)
    query_grad = jnp.einsum(
        "kgqs,skd->qkgd", score_grad, key_rows, preferred_element_type=jnp.float32
    )
    key_grad = jnp.einsum("kgqs,qkgd->skd", score_grad, queries, preferred_element_type=jnp.float32)
    value_grad = jnp.einsum(
        "kgqs,qkgd->skd",
        attention_again.astype(jnp.bfloat16),
        attended_grad,
        preferred_element_type=jnp.float32,
    )
    query_lin_grad = rotate(query_grad.reshape(seq_len, HEADS, HEAD_DIM), cosine, -sine_table)
    query_lin_grad = query_lin_grad.reshape(seq_len, HEADS * HEAD_DIM).astype(jnp.bfloat16)
    key_lin_grad = rotate(key_grad, cosine, -sine_table).reshape(seq_len, kv_cols)
    keyval_lin_grad = jnp.concatenate(
        [key_lin_grad, value_grad.reshape(seq_len, kv_cols)], axis=1
    ).astype(jnp.bfloat16)
    grad_query = jnp.dot(act_one.T, query_lin_grad, preferred_element_type=jnp.float32)
    grad_keyval = jnp.dot(act_one.T, keyval_lin_grad, preferred_element_type=jnp.float32)
    act_one_grad = jnp.dot(query_lin_grad, query_all.T, preferred_element_type=jnp.float32)
    act_one_grad = act_one_grad + jnp.dot(
        keyval_lin_grad, keyval_all.T, preferred_element_type=jnp.float32
    )
    norm_grad_one, grad_gain_one = norm_back(act_one_grad, normed_one, inverse_one, gain_one_f)
    grad_tokens = hidden_grad + norm_grad_one
    small_grad = jnp.concatenate(
        [
            grad_router,
            grad_gain_one[:, None],
            grad_gain_two[:, None],
            jnp.zeros((width_model, 128 - EXPERTS - 2), jnp.float32),
        ],
        axis=1,
    )
    blocks = [
        each.astype(jnp.bfloat16).reshape(dp_count, count, -1, each.shape[1])
        for each in (grad_output_w, grad_keyval, grad_query, small_grad)
    ]
    sum_output, sum_keyval, sum_query, sum_small, late_sum = shared_stage(
        blocks, raw, late, count, dp_count
    )
    sum_output, sum_keyval, sum_query, sum_small = (
        each.reshape(-1, each.shape[-1]) for each in (sum_output, sum_keyval, sum_query, sum_small)
    )
    sums = jnp.concatenate([early_sum, late_sum], axis=0) if late else early_sum
    up_rows = width_model // dp_count
    return (
        output,
        grad_tokens,
        sum_query,
        sum_keyval,
        sum_output,
        sum_small[:, :EXPERTS],
        sum_small[:, EXPERTS],
        sum_small[:, EXPERTS + 1],
        sums[:, :, :, :up_rows].astype(jnp.float32).reshape(w_gate_up.shape),
        sums[:, :, :, up_rows:].astype(jnp.float32).reshape(w_down.shape),
    )


def solution(mesh):
    return jax.shard_map(
        shards,
        mesh=mesh,
        in_specs=(
            P(("dp", "expert"), None),
            P(("dp", "expert"), None),
            P(("dp", "expert"), None),
            P(("dp", "expert"), None),
            P(("dp", "expert"), None),
            P("dp", None),
            P("dp", None),
            P("dp", None),
            P("dp", None),
            P("dp"),
            P("dp"),
            P("expert", None, None),
            P("expert", None, None),
        ),
        out_specs=(
            P(("dp", "expert"), None),
            P(("dp", "expert"), None),
            P("dp", None),
            P("dp", None),
            P("dp", None),
            P("dp", None),
            P("dp"),
            P("dp"),
            P("expert", None, None),
            P("expert", None, None),
        ),
        check_vma=False,
    )
```
